32 devices in a mesh: frame: 4 (over y, x), row: 8 (over z, core).
Axes of the slice: x: 2, y: 2, z: 4, core: 2. Of those that a mesh axis runs over, the one named last changes fastest.
Arguments:
- frames_in: bfloat16 [8, 32, 32, 256], P('frame', 'row'), may hold values from -6 to 6
- conv_first: bfloat16 [3, 3, 256, 256], replicated, may hold values from -0.125 to 0.125
- conv_second: bfloat16 [3, 3, 256, 256], replicated, may hold values from -0.125 to 0.125
- time_kernel: bfloat16 [3, 256, 256], replicated, may hold values from -0.21875 to 0.21875
- norm_gain: float32 [256], replicated, may hold values from 0.1 to 1.9
- w_query: bfloat16 [256, 256], replicated, may hold values from -0.375 to 0.375
- w_key: bfloat16 [256, 256], replicated, may hold values from -0.375 to 0.375
- w_value: bfloat16 [256, 256], replicated, may hold values from -0.375 to 0.375
- w_out: bfloat16 [256, 256], replicated, may hold values from -0.375 to 0.375
- frame_bias: float32 [8, 8], replicated, may hold values from -6 to 400
- conv_third: bfloat16 [3, 3, 256, 256], replicated, may hold values from -0.125 to 0.125
Outputs:
- encoded: bfloat16 [8, 32, 32, 256], P(None, 'row', 'frame')
The draws below stay inside these ranges and needn't reach their ends.
All inputs are finite; a program needn't handle non-finite values.
Results may differ from the reference program's by a relative error of at most 0.018.
Values may be sent and summed in bfloat16 or wider, within the bound.
A program may use at most 64 MiB of HBM per device.

```python
import math
import jax
import jax.numpy as jnp
from jax import lax

C = 256
FRAMES = 8
HEIGHT = 32
WIDTH = 32


def draw_frame_bias(key, part):
    drawn = jnp.clip(jax.random.normal(key, (FRAMES, FRAMES), jnp.float32), -6.0, 6.0)
    return drawn


def level_of(key, shape, pieces, low, largest):
    loudness = 1.0
    for dim, parts in pieces:
        draws = jax.random.uniform(jax.random.fold_in(jax.random.fold_in(key, 6), dim), (parts,), jnp.float32, low / len(pieces), largest / len(pieces))
        loudness = loudness * jnp.repeat(jnp.exp(draws), shape[dim] // parts).reshape((-1,) + (1,) * (len(shape) - 1 - dim))
    return loudness


def scatter_about(key, dims, deviation, reach, split=(), held_as=jnp.bfloat16):
    values = deviation * jax.random.normal(key, dims, jnp.float32)
    if split:
        values = values * level_of(key, dims, split, -0.22, 0.18)
    return jnp.clip(values, -reach, reach).astype(held_as)


def setup_inputs(seed: int = 0) -> dict:
    arg_keys = jax.random.split(jax.random.key(seed), 12)
    frames_in = scatter_about(arg_keys[0], (FRAMES, HEIGHT, WIDTH, C), 1.0, 6.0, ((0, 4), (1, 8)))
    conv_first = scatter_about(arg_keys[1], (3, 3, C, C), (9 * C) ** -0.5, 0.125)
    conv_second = scatter_about(arg_keys[2], (3, 3, C, C), (9 * C) ** -0.5, 0.125)
    time_kernel = scatter_about(arg_keys[3], (3, C, C), (3 * C) ** -0.5, 0.21875)
    norm_gain = jnp.clip(1.0 + 0.18 * jax.random.normal(arg_keys[4], (C,), jnp.float32), 0.1, 1.9)
    w_query = scatter_about(arg_keys[5], (C, C), C ** -0.5, 0.375)
    w_key = scatter_about(arg_keys[6], (C, C), C ** -0.5, 0.375)
    w_value = scatter_about(arg_keys[7], (C, C), C ** -0.5, 0.375)
    w_out = scatter_about(arg_keys[8], (C, C), C ** -0.5, 0.375)
    frame_bias = draw_frame_bias(jax.random.fold_in(arg_keys[11], 71), 0)
    conv_third = scatter_about(arg_keys[10], (3, 3, C, C), (9 * C) ** -0.5, 0.125)
    return {"frames_in": frames_in, "conv_first": conv_first, "conv_second": conv_second, "time_kernel": time_kernel, "norm_gain": norm_gain, "w_query": w_query, "w_key": w_key, "w_value": w_value, "w_out": w_out, "frame_bias": frame_bias, "conv_third": conv_third}


def spatial(padded, weight, row_count, col_count):
    channels = weight.shape[2]
    summed = jnp.zeros((padded.shape[0] * row_count * col_count, weight.shape[3]), jnp.float32)
    for row_tap in range(3):
        for col_tap in range(3):
            window = padded[:, row_tap:row_tap + row_count, col_tap:col_tap + col_count, :]
            summed = summed + jnp.dot(window.reshape(-1, channels), weight[row_tap, col_tap], preferred_element_type=jnp.float32)
    return summed.reshape(padded.shape[0], row_count, col_count, weight.shape[3])

def pad_image(field):
    return jnp.pad(field, ((0, 0), (1, 1), (1, 1), (0, 0)))

def temporal(moved, time_kernel, norm_gain, w_query, w_key, w_value, w_out, frame_bias):
    frame_count = moved.shape[0]
    channels = moved.shape[-1]
    pixels = moved.reshape(frame_count, -1, channels)
    padded = jnp.pad(pixels, ((1, 1), (0, 0), (0, 0)))
    summed = pixels.astype(jnp.float32)
    for tap in range(3):
        shifted = padded[tap:tap + frame_count].reshape(-1, channels)
        summed = summed + jnp.dot(shifted, time_kernel[tap], preferred_element_type=jnp.float32).reshape(pixels.shape)
    timed = summed.astype(jnp.bfloat16)
    widened = timed.astype(jnp.float32)
    scale_inv = lax.rsqrt(lax.optimization_barrier(jnp.mean(widened * widened, axis=-1, keepdims=True)) + 1e-06)
    normed = (widened * scale_inv * norm_gain.astype(jnp.float32)).astype(jnp.bfloat16).reshape(-1, channels)
    queries = jnp.dot(normed, w_query, preferred_element_type=jnp.float32).astype(jnp.bfloat16).reshape(pixels.shape)
    key_rows = jnp.dot(normed, w_key, preferred_element_type=jnp.float32).astype(jnp.bfloat16).reshape(pixels.shape)
    value_rows = jnp.dot(normed, w_value, preferred_element_type=jnp.float32).astype(jnp.bfloat16).reshape(pixels.shape)
    scores = jnp.einsum('fpc,gpc->pfg', queries.astype(jnp.float32), key_rows.astype(jnp.float32)) / math.sqrt(channels)
    scores = scores + frame_bias.astype(jnp.float32)
    peak = lax.optimization_barrier(jnp.max(scores, axis=-1, keepdims=True))
    raised = jnp.exp(scores - peak)
    probs = (raised / lax.optimization_barrier(jnp.sum(raised, axis=-1, keepdims=True))).astype(jnp.bfloat16)
    context = jnp.einsum('pfg,gpc->fpc', probs.astype(jnp.float32), value_rows.astype(jnp.float32)).astype(jnp.bfloat16)
    projected = jnp.dot(context.reshape(-1, channels), w_out, preferred_element_type=jnp.float32).reshape(pixels.shape)
    return (widened + projected).astype(jnp.bfloat16).reshape(moved.shape)

def reference(frames_in, conv_first, conv_second, time_kernel, norm_gain, w_query, w_key, w_value, w_out, frame_bias, conv_third):
    row_count = frames_in.shape[1]
    col_count = frames_in.shape[2]
    first = jax.nn.silu(spatial(pad_image(frames_in), conv_first, row_count, col_count)).astype(jnp.bfloat16)
    second = jax.nn.silu(spatial(pad_image(first), conv_second, row_count, col_count)).astype(jnp.bfloat16)
    attended = temporal(second, time_kernel, norm_gain, w_query, w_key, w_value, w_out, frame_bias)
    return spatial(pad_image(attended), conv_third, row_count, col_count).astype(jnp.bfloat16)
```

```python
import functools
import math

import jax
import jax.numpy as jnp
from jax import lax
from jax.experimental import pallas as pl
from jax.experimental.pallas import tpu as pltpu
from jax.sharding import PartitionSpec as P

MESH = pl.DeviceIdType.MESH
BF16 = jnp.bfloat16
F32 = jnp.float32
HALO = 3
GROUP = 16


def matmul(lhs, rhs):
    return jnp.dot(lhs, rhs, preferred_element_type=F32)


def silu(v):
    return 0.5 * v * (1.0 + jnp.tanh(0.5 * v))


def steps_below(index, pitch, count):
    quotient = jnp.zeros_like(index)
    for k in range(1, count):
        quotient = quotient + (index >= k * pitch).astype(jnp.int32)
    return quotient


def shifted_columns(rows, width):
    count, _, channels = rows.shape
    flat = rows.astype(F32).reshape(count * width, channels)
    column = lax.broadcasted_iota(jnp.int32, (count, width, channels), 1)
    left = pltpu.roll(flat, 1, 0).reshape(count, width, channels)
    right = pltpu.roll(flat, count * width - 1, 0).reshape(count, width, channels)
    left = jnp.where(column == 0, 0.0, left).astype(BF16)
    right = jnp.where(column == width - 1, 0.0, right).astype(BF16)
    return left, right


def kernel(
    frames_axis,
    rows_axis,
    x_hbm,
    w1_hbm,
    w2_hbm,
    tk_hbm,
    gain_ref,
    wq_hbm,
    wk_hbm,
    wv_hbm,
    wo_hbm,
    bias_ref,
    w3_hbm,
    out_ref,
    xin,
    xs,
    fs,
    w1,
    w2,
    tk,
    wq,
    wk,
    wv,
    wo,
    w3,
    pick,
    packed,
    moved,
    context,
    cols3,
    local_sem,
    halo_send,
    halo_recv,
    send_sem,
    recv_sem,
):
    frame = lax.axis_index("frame")
    row = lax.axis_index("row")
    local_frames, row_count, width, channels = x_hbm.shape
    frame_count = frames_axis * local_frames
    cols = width // frames_axis
    pitch = cols + 2
    tile_rows = row_count + 2
    slots = packed.shape[2]
    height = row_count * rows_axis

    own = pltpu.make_async_copy(x_hbm, xin.at[:, HALO : HALO + row_count], local_sem.at[0])
    own.start()
    loads = []
    for k, (src, dst) in enumerate(
        ((w1_hbm, w1), (w2_hbm, w2), (tk_hbm, tk), (wq_hbm, wq), (wk_hbm, wk), (wv_hbm, wv), (wo_hbm, wo), (w3_hbm, w3))
    ):
        load = pltpu.make_async_copy(src, dst, local_sem.at[k + 1])
        load.start()
        loads.append(load)

    barrier = pltpu.get_barrier_semaphore()
    above = lax.rem(row + rows_axis - 1, rows_axis)
    below = lax.rem(row + 1, rows_axis)

    @pl.when(row > 0)
    def _():
        pl.semaphore_signal(barrier, inc=1, device_id={"row": above}, device_id_type=MESH)

    @pl.when(row < rows_axis - 1)
    def _():
        pl.semaphore_signal(barrier, inc=1, device_id={"row": below}, device_id_type=MESH)

    for k in range(1, frames_axis):
        peer = lax.rem(frame + k, frames_axis)
        pl.semaphore_signal(barrier, inc=1, device_id={"frame": peer}, device_id_type=MESH)
    neighbours = (row > 0).astype(jnp.int32) + (row < rows_axis - 1).astype(jnp.int32)
    pl.semaphore_wait(barrier, neighbours + (frames_axis - 1))

    up = pltpu.make_async_remote_copy(
        src_ref=x_hbm.at[:, 0:HALO],
        dst_ref=xin.at[:, HALO + row_count : 2 * HALO + row_count],
        send_sem=halo_send.at[1],
        recv_sem=halo_recv.at[1],
        device_id={"row": above},
        device_id_type=MESH,
    )
    down = pltpu.make_async_remote_copy(
        src_ref=x_hbm.at[:, row_count - HALO : row_count],
        dst_ref=xin.at[:, 0:HALO],
        send_sem=halo_send.at[0],
        recv_sem=halo_recv.at[0],
        device_id={"row": below},
        device_id_type=MESH,
    )

    @pl.when(row > 0)
    def _():
        up.start()

    @pl.when(row < rows_axis - 1)
    def _():
        down.start()

    blank = jnp.zeros((local_frames, HALO, width, channels), BF16)

    @pl.when(row == 0)
    def _():
        xin[:, 0:HALO] = blank

    @pl.when(row == rows_axis - 1)
    def _():
        xin[:, HALO + row_count : 2 * HALO + row_count] = blank

    target = lax.broadcasted_iota(jnp.int32, (frames_axis * slots, tile_rows * width), 0)
    source = lax.broadcasted_iota(jnp.int32, (frames_axis * slots, tile_rows * width), 1)
    owner = steps_below(target, slots, frames_axis)
    slot = target - owner * slots
    slot_row = steps_below(slot, pitch, tile_rows)
    slot_col = slot - slot_row * pitch + owner * cols - 1
    wanted = slot_row * width + slot_col
    taken = (
        (slot < tile_rows * pitch) & (slot_col >= 0) & (slot_col < width) & (source == wanted)
    )
    pick[...] = jnp.where(taken, 1.0, 0.0).astype(BF16)
    edge = jnp.zeros((1, slots, channels), BF16)
    moved[0:1] = edge
    moved[frame_count + 1 : frame_count + 2] = edge

    def spread(first_row, last_row):
        for f in range(local_frames):
            rows = xin[f, first_row:last_row]
            left, right = shifted_columns(rows, width)
            xs[f, first_row:last_row, :, 0:channels] = left
            xs[f, first_row:last_row, :, channels : 2 * channels] = rows
            xs[f, first_row:last_row, :, 2 * channels : 3 * channels] = right

    own.wait()
    spread(HALO, HALO + row_count)
    loads[0].wait()

    @pl.when(row > 0)
    def _():
        down.wait_recv()

    @pl.when(row < rows_axis - 1)
    def _():
        up.wait_recv()

    spread(0, HALO)
    spread(HALO + row_count, 2 * HALO + row_count)

    first_rows = row_count + 4
    image_row = (
        lax.broadcasted_iota(jnp.int32, (first_rows, width, channels), 0) + row * row_count - 2
    )
    first_in = (image_row >= 0) & (image_row < height)
    image_row = (
        lax.broadcasted_iota(jnp.int32, (tile_rows, width, channels), 0) + row * row_count - 1
    )
    second_in = (image_row >= 0) & (image_row < height)
    for f in range(local_frames):
        summed = None
        for a in range(3):
            part = matmul(
                xs[f, a : a + first_rows].reshape(first_rows * width, 3 * channels),
                w1[a].reshape(3 * channels, channels),
            )
            summed = part if summed is None else summed + part
        first = silu(summed).reshape(first_rows, width, channels)
        first = jnp.where(first_in, first, 0.0).astype(BF16)
        left, right = shifted_columns(first, width)
        fs[f, :, :, 0:channels] = left
        fs[f, :, :, channels : 2 * channels] = first
        fs[f, :, :, 2 * channels : 3 * channels] = right

    loads[1].wait()
    exchanges = []
    for f in range(local_frames):
        summed = None
        for a in range(3):
            part = matmul(
                fs[f, a : a + tile_rows].reshape(tile_rows * width, 3 * channels),
                w2[a].reshape(3 * channels, channels),
            )
            summed = part if summed is None else summed + part
        second = silu(summed).reshape(tile_rows, width, channels)
        second = jnp.where(second_in, second, 0.0).astype(BF16).reshape(tile_rows * width, channels)
        packed[f] = matmul(pick[...], second).astype(BF16).reshape(frames_axis, slots, channels)
        for k in range(1, frames_axis):
            peer = lax.rem(frame + k, frames_axis)
            exchange = pltpu.make_async_remote_copy(
                src_ref=packed.at[f, peer],
                dst_ref=moved.at[1 + frame * local_frames + f],
                send_sem=send_sem.at[f, k],
                recv_sem=recv_sem.at[f, k],
                device_id={"frame": peer},
                device_id_type=MESH,
            )
            exchange.start()
            exchanges.append(exchange)
        moved[1 + frame * local_frames + f] = packed[f, frame]

    span = frame_count * GROUP
    lane = lax.broadcasted_iota(jnp.int32, (frame_count, span), 1)
    wide = jnp.zeros((frame_count, span), F32)
    for g in range(frame_count):
        inside = (lane >= g * GROUP) & (lane < (g + 1) * GROUP)
        wide = jnp.where(inside, bias_ref[:, g : g + 1], wide)
    wide = jnp.broadcast_to(wide[:, None, :], (frame_count, GROUP, span)).reshape(span, span)
    query_pixel = jnp.bitwise_and(lax.broadcasted_iota(jnp.int32, (span, span), 0), GROUP - 1)
    key_pixel = jnp.bitwise_and(lax.broadcasted_iota(jnp.int32, (span, span), 1), GROUP - 1)
    masked_bias = jnp.where(query_pixel == key_pixel, wide, -1e30)

    taps = tile_rows * cols
    target = lax.broadcasted_iota(jnp.int32, (3 * taps, slots), 0)
    source = lax.broadcasted_iota(jnp.int32, (3 * taps, slots), 1)
    shift = steps_below(target, taps, 3)
    inner = target - shift * taps
    inner_row = steps_below(inner, cols, tile_rows)
    wanted = inner_row * pitch + inner - inner_row * cols + shift
    pick3 = jnp.where(source == wanted, 1.0, 0.0).astype(BF16)

    for load in loads[2:]:
        load.wait()
    for exchange in exchanges:
        exchange.wait_recv()

    pixels = frame_count * slots
    centre = moved[1 : 1 + frame_count].reshape(pixels, channels)
    summed = centre.astype(F32)
    for tap in range(3):
        summed = summed + matmul(moved[tap : tap + frame_count].reshape(pixels, channels), tk[tap])
    timed = summed.astype(BF16)
    widened = timed.astype(F32)
    scale_inv = lax.rsqrt(jnp.mean(widened * widened, axis=-1, keepdims=True) + 1e-06)
    normed = (widened * scale_inv * gain_ref[...]).astype(BF16)
    tile = (frame_count, slots, channels)
    queries = matmul(normed, wq[...]).astype(BF16).reshape(tile)
    key_rows = matmul(normed, wk[...]).astype(BF16).reshape(tile)
    value_rows = matmul(normed, wv[...]).astype(BF16).reshape(tile)
    for g in range(slots // GROUP):
        part = slice(g * GROUP, (g + 1) * GROUP)
        scores = lax.dot_general(
            queries[:, part].reshape(span, channels),
            key_rows[:, part].reshape(span, channels),
            (((1,), (1,)), ((), ())),
            preferred_element_type=F32,
        )
        scores = scores * (1.0 / math.sqrt(channels)) + masked_bias
        raised = jnp.exp(scores - jnp.max(scores, axis=-1, keepdims=True))
        probs = (raised / jnp.sum(raised, axis=-1, keepdims=True)).astype(BF16)
        mixed = matmul(probs, value_rows[:, part].reshape(span, channels))
        context[:, part] = mixed.astype(BF16).reshape(frame_count, GROUP, channels)
    attended = widened + matmul(context[...].reshape(pixels, channels), wo[...])
    attended = attended.astype(BF16).reshape(tile)

    count = row_count * cols
    for f in range(frame_count):
        gathered = matmul(pick3, attended[f])
        for a in range(3):
            for b in range(3):
                start = b * taps + a * cols
                cols3[a, f, :, b * channels : (b + 1) * channels] = gathered[
                    start : start + count
                ].astype(BF16)
    summed = None
    for a in range(3):
        part = matmul(
            cols3[a].reshape(frame_count * count, 3 * channels),
            w3[a].reshape(3 * channels, channels),
        )
        summed = part if summed is None else summed + part
    out_ref[...] = summed.reshape(frame_count, row_count, cols, channels).astype(BF16)

    @pl.when(row > 0)
    def _():
        up.wait_send()

    @pl.when(row < rows_axis - 1)
    def _():
        down.wait_send()

    for exchange in exchanges:
        exchange.wait_send()


def on_device(frames_axis, rows_axis, *args):
    frames_in = args[0]
    norm_gain = args[4]
    local_frames, row_count, width, channels = frames_in.shape
    frame_count = local_frames * frames_axis
    cols = width // frames_axis
    slots = -(-(row_count + 2) * (cols + 2) // GROUP) * GROUP
    args = args[:4] + (norm_gain.reshape(1, channels),) + args[5:]
    any_space = pl.BlockSpec(memory_space=pl.ANY)
    vmem = pl.BlockSpec(memory_space=pltpu.VMEM)
    weight = pltpu.VMEM((3, 3, channels, channels), BF16)
    square = pltpu.VMEM((channels, channels), BF16)
    return pl.pallas_call(
        functools.partial(kernel, frames_axis, rows_axis),
        out_shape=jax.ShapeDtypeStruct((frame_count, row_count, cols, channels), BF16),
        in_specs=[any_space] * 4 + [vmem] + [any_space] * 4 + [vmem, any_space],
        out_specs=vmem,
        scratch_shapes=[
            pltpu.VMEM((local_frames, row_count + 2 * HALO, width, channels), BF16),
            pltpu.VMEM((local_frames, row_count + 2 * HALO, width, 3 * channels), BF16),
            pltpu.VMEM((local_frames, row_count + 4, width, 3 * channels), BF16),
            weight,
            weight,
            pltpu.VMEM((3, channels, channels), BF16),
            square,
            square,
            square,
            square,
            weight,
            pltpu.VMEM((frames_axis * slots, (row_count + 2) * width), BF16),
            pltpu.VMEM((local_frames, frames_axis, slots, channels), BF16),
            pltpu.VMEM((frame_count + 2, slots, channels), BF16),
            pltpu.VMEM((frame_count, slots, channels), BF16),
            pltpu.VMEM((3, frame_count, row_count * cols, 3 * channels), BF16),
            pltpu.SemaphoreType.DMA((9,)),
            pltpu.SemaphoreType.DMA((2,)),
            pltpu.SemaphoreType.DMA((2,)),
            pltpu.SemaphoreType.DMA((local_frames, frames_axis)),
            pltpu.SemaphoreType.DMA((local_frames, frames_axis)),
        ],
        compiler_params=pltpu.CompilerParams(
            collective_id=0, has_side_effects=True, vmem_limit_bytes=56 * 1024 * 1024
        ),
    )(*args)


def solution(mesh):
    placed = (P("frame", "row", None, None),) + (P(),) * 10
    return jax.shard_map(
        functools.partial(on_device, mesh.shape["frame"], mesh.shape["row"]),
        mesh=mesh,
        in_specs=placed,
        out_specs=P(None, "row", "frame", None),
        check_vma=False,
    )
```

```python
import functools
import math

import jax
import jax.numpy as jnp
from jax import lax
from jax.experimental import pallas as pl
from jax.experimental.pallas import tpu as pltpu
from jax.sharding import PartitionSpec as P

MESH = pl.DeviceIdType.MESH
BF16 = jnp.bfloat16
F32 = jnp.float32
HALO = 3
GROUP = 16


def matmul(lhs, rhs):
    return jnp.dot(lhs, rhs, preferred_element_type=F32)


def silu(v):
    return 0.5 * v * (1.0 + jnp.tanh(0.5 * v))


def steps_below(index, pitch, count):
    quotient = jnp.zeros_like(index)
    for k in range(1, count):
        quotient = quotient + (index >= k * pitch).astype(jnp.int32)
    return quotient


def shifted_columns(rows, width):
    count, _, channels = rows.shape
    flat = rows.astype(F32).reshape(count * width, channels)
    column = lax.broadcasted_iota(jnp.int32, (count, width, channels), 1)
    left = pltpu.roll(flat, 1, 0).reshape(count, width, channels)
    right = pltpu.roll(flat, count * width - 1, 0).reshape(count, width, channels)
    left = jnp.where(column == 0, 0.0, left).astype(BF16)
    right = jnp.where(column == width - 1, 0.0, right).astype(BF16)
    return left, right


def kernel(
    frames_axis,
    rows_axis,
    x_hbm,
    w1_hbm,
    w2_hbm,
    tk_hbm,
    gain_hbm,
    wq_hbm,
    wk_hbm,
    wv_hbm,
    wo_hbm,
    bias_hbm,
    w3_hbm,
    out_ref,
    xin,
    xs,
    fs,
    w1,
    w2,
    tk,
    wq,
    wk,
    wv,
    wo,
    w3,
    partial,
    gain_ref,
    bias_ref,
    pick,
    packed,
    moved,
    context,
    cols3,
    local_sem,
    halo_send,
    halo_recv,
    send_sem,
    recv_sem,
):
    frame = lax.axis_index("frame")
    row = lax.axis_index("row")
    local_frames, row_count, width, channels = x_hbm.shape
    frame_count = frames_axis * local_frames
    cols = width // frames_axis
    pitch = cols + 2
    tile_rows = row_count + 2
    slots = packed.shape[2]
    height = row_count * rows_axis

    barrier = pltpu.get_barrier_semaphore()
    above = lax.rem(row + rows_axis - 1, rows_axis)
    below = lax.rem(row + 1, rows_axis)

    @pl.when(row > 0)
    def _():
        pl.semaphore_signal(barrier, inc=1, device_id={"row": above}, device_id_type=MESH)

    @pl.when(row < rows_axis - 1)
    def _():
        pl.semaphore_signal(barrier, inc=1, device_id={"row": below}, device_id_type=MESH)

    for k in range(1, frames_axis):
        peer = lax.rem(frame + k, frames_axis)
        pl.semaphore_signal(barrier, inc=1, device_id={"frame": peer}, device_id_type=MESH)
    own = pltpu.make_async_copy(x_hbm, xin.at[:, HALO : HALO + row_count], local_sem.at[0])
    own.start()
    loads = []
    for k, (src, dst) in enumerate(
        ((w1_hbm, w1), (w2_hbm, w2), (tk_hbm, tk), (wq_hbm, wq), (wk_hbm, wk), (wv_hbm, wv), (wo_hbm, wo), (gain_hbm, gain_ref), (bias_hbm, bias_ref), (w3_hbm, w3))
    ):
        load = pltpu.make_async_copy(src, dst, local_sem.at[k + 1])
        load.start()
        loads.append(load)

    neighbours = (row > 0).astype(jnp.int32) + (row < rows_axis - 1).astype(jnp.int32)
    pl.semaphore_wait(barrier, neighbours + (frames_axis - 1))

    ups, downs = [], []
    for f in range(local_frames):
        ups.append(
            pltpu.make_async_remote_copy(
                src_ref=x_hbm.at[f, 0:HALO],
                dst_ref=xin.at[f, HALO + row_count : 2 * HALO + row_count],
                send_sem=halo_send.at[f, 1],
                recv_sem=halo_recv.at[f, 1],
                device_id={"row": above},
                device_id_type=MESH,
            )
        )
        downs.append(
            pltpu.make_async_remote_copy(
                src_ref=x_hbm.at[f, row_count - HALO : row_count],
                dst_ref=xin.at[f, 0:HALO],
                send_sem=halo_send.at[f, 0],
                recv_sem=halo_recv.at[f, 0],
                device_id={"row": below},
                device_id_type=MESH,
            )
        )
    for up, down in zip(ups, downs):
        pl.when(row > 0)(up.start)
        pl.when(row < rows_axis - 1)(down.start)

    blank = jnp.zeros((local_frames, HALO, width, channels), BF16)

    @pl.when(row == 0)
    def _():
        xin[:, 0:HALO] = blank

    @pl.when(row == rows_axis - 1)
    def _():
        xin[:, HALO + row_count : 2 * HALO + row_count] = blank

    target = lax.broadcasted_iota(jnp.int32, (frames_axis * slots, tile_rows * width), 0)
    source = lax.broadcasted_iota(jnp.int32, (frames_axis * slots, tile_rows * width), 1)
    owner = steps_below(target, slots, frames_axis)
    slot = target - owner * slots
    slot_row = steps_below(slot, pitch, tile_rows)
    slot_col = slot - slot_row * pitch + owner * cols - 1
    wanted = slot_row * width + slot_col
    taken = (
        (slot < tile_rows * pitch) & (slot_col >= 0) & (slot_col < width) & (source == wanted)
    )
    pick[...] = jnp.where(taken, 1.0, 0.0).astype(BF16)
    edge = jnp.zeros((1, slots, channels), BF16)
    moved[0:1] = edge
    moved[frame_count + 1 : frame_count + 2] = edge

    def spread(f, first_row, last_row):
        rows = xin[f, first_row:last_row]
        left, right = shifted_columns(rows, width)
        xs[f, first_row:last_row, :, 0:channels] = left
        xs[f, first_row:last_row, :, channels : 2 * channels] = rows
        xs[f, first_row:last_row, :, 2 * channels : 3 * channels] = right

    own.wait()
    for f in range(local_frames):
        spread(f, HALO, HALO + row_count)
    loads[0].wait()

    own_part = (local_frames, row_count, width, channels)
    for i in (0, row_count + 3):
        partial[:, i] = jnp.zeros((local_frames, width, channels), F32)
    own_rows = xs[:, HALO : HALO + row_count].reshape(-1, 3 * channels)
    shares = [
        matmul(own_rows, w1[a].reshape(3 * channels, channels)).reshape(own_part) for a in range(3)
    ]
    for i in range(row_count + 4):
        terms = [shares[a][:, i + a - HALO] for a in range(3) if 0 <= i + a - HALO < row_count]
        if terms:
            partial[:, i] = functools.reduce(jnp.add, terms)

    first_rows = row_count + 4
    exchanges = []
    image_row = (
        lax.broadcasted_iota(jnp.int32, (first_rows, width, channels), 0) + row * row_count - 2
    )
    first_in = (image_row >= 0) & (image_row < height)
    image_row = (
        lax.broadcasted_iota(jnp.int32, (tile_rows, width, channels), 0) + row * row_count - 1
    )
    second_in = (image_row >= 0) & (image_row < height)
    for f in range(local_frames):
        pl.when(row > 0)(downs[f].wait_recv)
        pl.when(row < rows_axis - 1)(ups[f].wait_recv)
        spread(f, 0, HALO)
        spread(f, HALO + row_count, 2 * HALO + row_count)
        rows = [partial[f, i] for i in range(first_rows)]
        for a in range(3):
            edges = jnp.concatenate([xs[f, a:HALO], xs[f, HALO + row_count : first_rows + a]], axis=0)
            part = matmul(
                edges.reshape(-1, 3 * channels), w1[a].reshape(3 * channels, channels)
            ).reshape(-1, width, channels)
            reached = list(range(HALO - a)) + list(range(HALO + row_count - a, first_rows))
            for k, i in enumerate(reached):
                rows[i] = rows[i] + part[k]
        summed = jnp.concatenate(rows, axis=0)
        first = silu(summed).reshape(first_rows, width, channels)
        first = jnp.where(first_in, first, 0.0).astype(BF16)
        left, right = shifted_columns(first, width)
        fs[f, :, :, 0:channels] = left
        fs[f, :, :, channels : 2 * channels] = first
        fs[f, :, :, 2 * channels : 3 * channels] = right

        if f == 0:
            loads[1].wait()
        summed = None
        for a in range(3):
            part = matmul(
                fs[f, a : a + tile_rows].reshape(tile_rows * width, 3 * channels),
                w2[a].reshape(3 * channels, channels),
            )
            summed = part if summed is None else summed + part
        second = silu(summed).reshape(tile_rows, width, channels)
        second = jnp.where(second_in, second, 0.0).astype(BF16).reshape(tile_rows * width, channels)
        packed[f] = matmul(pick[...], second).astype(BF16).reshape(frames_axis, slots, channels)
        for k in range(1, frames_axis):
            peer = lax.rem(frame + k, frames_axis)
            exchange = pltpu.make_async_remote_copy(
                src_ref=packed.at[f, peer],
                dst_ref=moved.at[1 + frame * local_frames + f],
                send_sem=send_sem.at[f, k],
                recv_sem=recv_sem.at[f, k],
                device_id={"frame": peer},
                device_id_type=MESH,
            )
            exchange.start()
            exchanges.append(exchange)
        moved[1 + frame * local_frames + f] = packed[f, frame]

    for load in loads[2:]:
        load.wait()
    span = frame_count * GROUP
    lane = lax.broadcasted_iota(jnp.int32, (frame_count, span), 1)
    wide = jnp.zeros((frame_count, span), F32)
    for g in range(frame_count):
        inside = (lane >= g * GROUP) & (lane < (g + 1) * GROUP)
        wide = jnp.where(inside, bias_ref[:, g : g + 1], wide)
    wide = jnp.broadcast_to(wide[:, None, :], (frame_count, GROUP, span)).reshape(span, span)
    query_pixel = jnp.bitwise_and(lax.broadcasted_iota(jnp.int32, (span, span), 0), GROUP - 1)
    key_pixel = jnp.bitwise_and(lax.broadcasted_iota(jnp.int32, (span, span), 1), GROUP - 1)
    masked_bias = jnp.where(query_pixel == key_pixel, wide, -1e30)

    taps = tile_rows * cols
    target = lax.broadcasted_iota(jnp.int32, (3 * taps, slots), 0)
    source = lax.broadcasted_iota(jnp.int32, (3 * taps, slots), 1)
    shift = steps_below(target, taps, 3)
    inner = target - shift * taps
    inner_row = steps_below(inner, cols, tile_rows)
    wanted = inner_row * pitch + inner - inner_row * cols + shift
    pick3 = jnp.where(source == wanted, 1.0, 0.0).astype(BF16)

    for exchange in exchanges:
        exchange.wait_recv()

    pixels = frame_count * slots
    centre = moved[1 : 1 + frame_count].reshape(pixels, channels)
    summed = centre.astype(F32)
    for tap in range(3):
        summed = summed + matmul(moved[tap : tap + frame_count].reshape(pixels, channels), tk[tap])
    timed = summed.astype(BF16)
    widened = timed.astype(F32)
    scale_inv = lax.rsqrt(jnp.mean(widened * widened, axis=-1, keepdims=True) + 1e-06)
    normed = (widened * scale_inv * gain_ref[...]).astype(BF16)
    tile = (frame_count, slots, channels)
    queries = matmul(normed, wq[...]).astype(BF16).reshape(tile)
    key_rows = matmul(normed, wk[...]).astype(BF16).reshape(tile)
    value_rows = matmul(normed, wv[...]).astype(BF16).reshape(tile)
    for g in range(slots // GROUP):
        part = slice(g * GROUP, (g + 1) * GROUP)
        scores = lax.dot_general(
            queries[:, part].reshape(span, channels),
            key_rows[:, part].reshape(span, channels),
            (((1,), (1,)), ((), ())),
            preferred_element_type=F32,
        )
        scores = scores * (1.0 / math.sqrt(channels)) + masked_bias
        raised = jnp.exp(scores - jnp.max(scores, axis=-1, keepdims=True))
        probs = (raised / jnp.sum(raised, axis=-1, keepdims=True)).astype(BF16)
        mixed = matmul(probs, value_rows[:, part].reshape(span, channels))
        context[:, part] = mixed.astype(BF16).reshape(frame_count, GROUP, channels)
    attended = widened + matmul(context[...].reshape(pixels, channels), wo[...])
    attended = attended.astype(BF16).reshape(tile)

    count = row_count * cols
    for f in range(frame_count):
        gathered = matmul(pick3, attended[f])
        for a in range(3):
            for b in range(3):
                start = b * taps + a * cols
                cols3[a, f, :, b * channels : (b + 1) * channels] = gathered[
                    start : start + count
                ].astype(BF16)
    summed = None
    for a in range(3):
        part = matmul(
            cols3[a].reshape(frame_count * count, 3 * channels),
            w3[a].reshape(3 * channels, channels),
        )
        summed = part if summed is None else summed + part
    out_ref[...] = summed.reshape(frame_count, row_count, cols, channels).astype(BF16)

    for up, down in zip(ups, downs):
        pl.when(row > 0)(up.wait_send)
        pl.when(row < rows_axis - 1)(down.wait_send)
    for exchange in exchanges:
        exchange.wait_send()


def on_device(frames_axis, rows_axis, *args):
    frames_in = args[0]
    norm_gain = args[4]
    local_frames, row_count, width, channels = frames_in.shape
    frame_count = local_frames * frames_axis
    cols = width // frames_axis
    slots = -(-(row_count + 2) * (cols + 2) // GROUP) * GROUP
    args = args[:4] + (norm_gain.reshape(1, channels),) + args[5:]
    any_space = pl.BlockSpec(memory_space=pl.ANY)
    vmem = pl.BlockSpec(memory_space=pltpu.VMEM)
    weight = pltpu.VMEM((3, 3, channels, channels), BF16)
    square = pltpu.VMEM((channels, channels), BF16)
    return pl.pallas_call(
        functools.partial(kernel, frames_axis, rows_axis),
        out_shape=pltpu.VMEM((frame_count, row_count, cols, channels), BF16),
        in_specs=[any_space] * 11,
        out_specs=vmem,
        scratch_shapes=[
            pltpu.VMEM((local_frames, row_count + 2 * HALO, width, channels), BF16),
            pltpu.VMEM((local_frames, row_count + 2 * HALO, width, 3 * channels), BF16),
            pltpu.VMEM((local_frames, row_count + 4, width, 3 * channels), BF16),
            weight,
            weight,
            pltpu.VMEM((3, channels, channels), BF16),
            square,
            square,
            square,
            square,
            weight,
            pltpu.VMEM((local_frames, row_count + 4, width, channels), F32),
            pltpu.VMEM((1, channels), F32),
            pltpu.VMEM((frame_count, frame_count), F32),
            pltpu.VMEM((frames_axis * slots, (row_count + 2) * width), BF16),
            pltpu.VMEM((local_frames, frames_axis, slots, channels), BF16),
            pltpu.VMEM((frame_count + 2, slots, channels), BF16),
            pltpu.VMEM((frame_count, slots, channels), BF16),
            pltpu.VMEM((3, frame_count, row_count * cols, 3 * channels), BF16),
            pltpu.SemaphoreType.DMA((11,)),
            pltpu.SemaphoreType.DMA((local_frames, 2)),
            pltpu.SemaphoreType.DMA((local_frames, 2)),
            pltpu.SemaphoreType.DMA((local_frames, frames_axis)),
            pltpu.SemaphoreType.DMA((local_frames, frames_axis)),
        ],
        compiler_params=pltpu.CompilerParams(
            collective_id=0, has_side_effects=True, vmem_limit_bytes=56 * 1024 * 1024
        ),
    )(*args)


def solution(mesh):
    placed = (P("frame", "row", None, None),) + (P(),) * 10
    return jax.shard_map(
        functools.partial(on_device, mesh.shape["frame"], mesh.shape["row"]),
        mesh=mesh,
        in_specs=placed,
        out_specs=P(None, "row", "frame", None),
        check_vma=False,
    )
```

```python
import functools
import math

import jax
import jax.numpy as jnp
from jax import lax
from jax.experimental import pallas as pl
from jax.experimental.pallas import tpu as pltpu
from jax.sharding import PartitionSpec as P

MESH = pl.DeviceIdType.MESH
BF16 = jnp.bfloat16
F32 = jnp.float32
HALO = 3
GROUP = 16


def matmul(lhs, rhs):
    return jnp.dot(lhs, rhs, preferred_element_type=F32)


def partner(index, distance, count):
    if count & (count - 1):
        return lax.rem(index + distance, count)
    bit = 1
    while bit < count:
        if distance & bit:
            index = index + bit - 2 * bit * lax.rem(lax.div(index, bit), 2)
        bit *= 2
    return index


def silu(v):
    return 0.5 * v * (1.0 + jnp.tanh(0.5 * v))


def steps_below(index, pitch, count):
    quotient = jnp.zeros_like(index)
    for k in range(1, count):
        quotient = quotient + (index >= k * pitch).astype(jnp.int32)
    return quotient


def shifted_columns(rows, width):
    count, _, channels = rows.shape
    flat = rows.astype(F32).reshape(count * width, channels)
    column = lax.broadcasted_iota(jnp.int32, (count, width, channels), 1)
    left = pltpu.roll(flat, 1, 0).reshape(count, width, channels)
    right = pltpu.roll(flat, count * width - 1, 0).reshape(count, width, channels)
    left = jnp.where(column == 0, 0.0, left).astype(BF16)
    right = jnp.where(column == width - 1, 0.0, right).astype(BF16)
    return left, right


def kernel(
    frames_axis,
    rows_axis,
    x_hbm,
    w1_hbm,
    w2_hbm,
    tk_hbm,
    gain_hbm,
    wq_hbm,
    wk_hbm,
    wv_hbm,
    wo_hbm,
    bias_hbm,
    w3_hbm,
    out_ref,
    xin,
    xs,
    fs,
    w1,
    w2,
    tk,
    wq,
    wk,
    wv,
    wo,
    w3,
    partial,
    gain_ref,
    bias_ref,
    pick,
    packed,
    moved,
    context,
    cols3,
    local_sem,
    halo_send,
    halo_recv,
    send_sem,
    recv_sem,
):
    frame = lax.axis_index("frame")
    row = lax.axis_index("row")
    local_frames, row_count, width, channels = x_hbm.shape
    frame_count = frames_axis * local_frames
    cols = width // frames_axis
    pitch = cols + 2
    tile_rows = row_count + 2
    slots = packed.shape[2]
    height = row_count * rows_axis

    barrier = pltpu.get_barrier_semaphore()
    above = lax.rem(row + rows_axis - 1, rows_axis)
    below = lax.rem(row + 1, rows_axis)

    @pl.when(row > 0)
    def _():
        pl.semaphore_signal(barrier, inc=1, device_id={"row": above}, device_id_type=MESH)

    @pl.when(row < rows_axis - 1)
    def _():
        pl.semaphore_signal(barrier, inc=1, device_id={"row": below}, device_id_type=MESH)

    for k in range(1, frames_axis):
        peer = lax.rem(frame + k, frames_axis)
        pl.semaphore_signal(barrier, inc=1, device_id={"frame": peer}, device_id_type=MESH)
    own = pltpu.make_async_copy(x_hbm, xin.at[:, HALO : HALO + row_count], local_sem.at[0])
    own.start()
    loads = []
    for k, (src, dst) in enumerate(
        ((w1_hbm, w1), (w2_hbm, w2), (tk_hbm, tk), (wq_hbm, wq), (wk_hbm, wk), (wv_hbm, wv), (wo_hbm, wo), (gain_hbm, gain_ref), (bias_hbm, bias_ref), (w3_hbm, w3))
    ):
        load = pltpu.make_async_copy(src, dst, local_sem.at[k + 1])
        load.start()
        loads.append(load)

    neighbours = (row > 0).astype(jnp.int32) + (row < rows_axis - 1).astype(jnp.int32)
    pl.semaphore_wait(barrier, neighbours + (frames_axis - 1))

    ups, downs = [], []
    for f in range(local_frames):
        ups.append(
            pltpu.make_async_remote_copy(
                src_ref=xin.at[f, HALO : 2 * HALO],
                dst_ref=xin.at[f, HALO + row_count : 2 * HALO + row_count],
                send_sem=halo_send.at[f, 1],
                recv_sem=halo_recv.at[f, 1],
                device_id={"row": above},
                device_id_type=MESH,
            )
        )
        downs.append(
            pltpu.make_async_remote_copy(
                src_ref=xin.at[f, row_count : row_count + HALO],
                dst_ref=xin.at[f, 0:HALO],
                send_sem=halo_send.at[f, 0],
                recv_sem=halo_recv.at[f, 0],
                device_id={"row": below},
                device_id_type=MESH,
            )
        )
    own.wait()
    for up, down in zip(ups, downs):
        pl.when(row > 0)(up.start)
        pl.when(row < rows_axis - 1)(down.start)

    blank = jnp.zeros((local_frames, HALO, width, channels), BF16)

    @pl.when(row == 0)
    def _():
        xin[:, 0:HALO] = blank

    @pl.when(row == rows_axis - 1)
    def _():
        xin[:, HALO + row_count : 2 * HALO + row_count] = blank

    target = lax.broadcasted_iota(jnp.int32, (frames_axis * slots, tile_rows * width), 0)
    source = lax.broadcasted_iota(jnp.int32, (frames_axis * slots, tile_rows * width), 1)
    owner = steps_below(target, slots, frames_axis)
    slot = target - owner * slots
    inner_slots = tile_rows * cols
    slot_row = steps_below(slot, cols, tile_rows)
    slot_col = slot - slot_row * cols
    side = (slot >= inner_slots + tile_rows).astype(jnp.int32)
    outer = slot >= inner_slots
    slot_row = jnp.where(outer, slot - inner_slots - side * tile_rows, slot_row)
    slot_col = jnp.where(outer, side * (cols + 1) - 1, slot_col) + owner * cols
    wanted = slot_row * width + slot_col
    taken = (
        (slot < tile_rows * pitch) & (slot_col >= 0) & (slot_col < width) & (source == wanted)
    )
    pick[...] = jnp.where(taken, 1.0, 0.0).astype(BF16)
    edge = jnp.zeros((1, slots, channels), BF16)
    moved[0:1] = edge
    moved[frame_count + 1 : frame_count + 2] = edge

    def spread(f, first_row, last_row):
        rows = xin[f, first_row:last_row]
        left, right = shifted_columns(rows, width)
        xs[f, first_row:last_row, :, 0:channels] = left
        xs[f, first_row:last_row, :, channels : 2 * channels] = rows
        xs[f, first_row:last_row, :, 2 * channels : 3 * channels] = right

    for f in range(local_frames):
        spread(f, HALO, HALO + row_count)
    loads[0].wait()

    own_part = (local_frames, row_count, width, channels)
    for i in (0, row_count + 3):
        partial[:, i] = jnp.zeros((local_frames, width, channels), F32)
    own_rows = xs[:, HALO : HALO + row_count].reshape(-1, 3 * channels)
    shares = [
        matmul(own_rows, w1[a].reshape(3 * channels, channels)).reshape(own_part) for a in range(3)
    ]
    for i in range(row_count + 4):
        terms = [shares[a][:, i + a - HALO] for a in range(3) if 0 <= i + a - HALO < row_count]
        if terms:
            partial[:, i] = functools.reduce(jnp.add, terms)

    first_rows = row_count + 4
    exchanges = []
    image_row = (
        lax.broadcasted_iota(jnp.int32, (first_rows, width, channels), 0) + row * row_count - 2
    )
    first_in = (image_row >= 0) & (image_row < height)
    image_row = (
        lax.broadcasted_iota(jnp.int32, (tile_rows, width, channels), 0) + row * row_count - 1
    )
    second_in = (image_row >= 0) & (image_row < height)
    for f in range(local_frames):
        pl.when(row > 0)(downs[f].wait_recv)
        pl.when(row < rows_axis - 1)(ups[f].wait_recv)
        spread(f, 0, HALO)
        spread(f, HALO + row_count, 2 * HALO + row_count)
        rows = [partial[f, i] for i in range(first_rows)]
        for a in range(3):
            edges = jnp.concatenate([xs[f, a:HALO], xs[f, HALO + row_count : first_rows + a]], axis=0)
            part = matmul(
                edges.reshape(-1, 3 * channels), w1[a].reshape(3 * channels, channels)
            ).reshape(-1, width, channels)
            reached = list(range(HALO - a)) + list(range(HALO + row_count - a, first_rows))
            for k, i in enumerate(reached):
                rows[i] = rows[i] + part[k]
        summed = jnp.concatenate(rows, axis=0)
        first = silu(summed).reshape(first_rows, width, channels)
        first = jnp.where(first_in, first, 0.0).astype(BF16)
        left, right = shifted_columns(first, width)
        fs[f, :, :, 0:channels] = left
        fs[f, :, :, channels : 2 * channels] = first
        fs[f, :, :, 2 * channels : 3 * channels] = right

        if f == 0:
            loads[1].wait()
        summed = None
        for a in range(3):
            part = matmul(
                fs[f, a : a + tile_rows].reshape(tile_rows * width, 3 * channels),
                w2[a].reshape(3 * channels, channels),
            )
            summed = part if summed is None else summed + part
        second = silu(summed).reshape(tile_rows, width, channels)
        second = jnp.where(second_in, second, 0.0).astype(BF16).reshape(tile_rows * width, channels)
        packed[f] = matmul(pick[...], second).astype(BF16).reshape(frames_axis, slots, channels)
        for k in reversed(range(1, frames_axis)):
            peer = partner(frame, k, frames_axis)
            exchange = pltpu.make_async_remote_copy(
                src_ref=packed.at[f, peer],
                dst_ref=moved.at[1 + frame * local_frames + f],
                send_sem=send_sem.at[f, k],
                recv_sem=recv_sem.at[f, k],
                device_id={"frame": peer},
                device_id_type=MESH,
            )
            exchange.start()
            exchanges.append(exchange)
        moved[1 + frame * local_frames + f] = packed[f, frame]

    for load in loads[2:]:
        load.wait()
    span = frame_count * GROUP
    lane = lax.broadcasted_iota(jnp.int32, (frame_count, span), 1)
    wide = jnp.zeros((frame_count, span), F32)
    for g in range(frame_count):
        inside = (lane >= g * GROUP) & (lane < (g + 1) * GROUP)
        wide = jnp.where(inside, bias_ref[:, g : g + 1], wide)
    wide = jnp.broadcast_to(wide[:, None, :], (frame_count, GROUP, span)).reshape(span, span)
    query_pixel = jnp.bitwise_and(lax.broadcasted_iota(jnp.int32, (span, span), 0), GROUP - 1)
    key_pixel = jnp.bitwise_and(lax.broadcasted_iota(jnp.int32, (span, span), 1), GROUP - 1)
    masked_bias = jnp.where(query_pixel == key_pixel, wide, -1e30)

    taps = tile_rows * cols
    target = lax.broadcasted_iota(jnp.int32, (2 * taps, slots), 0)
    source = lax.broadcasted_iota(jnp.int32, (2 * taps, slots), 1)
    shift = (target >= taps).astype(jnp.int32)
    inner = target - shift * taps
    inner_row = steps_below(inner, cols, tile_rows)
    inner_col = inner - inner_row * cols
    outer = inner_col == shift * (cols - 1)
    wanted = jnp.where(outer, taps + shift * tile_rows + inner_row, inner + 2 * shift - 1)
    pick3 = jnp.where(source == wanted, 1.0, 0.0).astype(BF16)

    for exchange in exchanges:
        exchange.wait_recv()

    pixels = frame_count * slots
    centre = moved[1 : 1 + frame_count].reshape(pixels, channels)
    summed = centre.astype(F32)
    for tap in range(3):
        summed = summed + matmul(moved[tap : tap + frame_count].reshape(pixels, channels), tk[tap])
    timed = summed.astype(BF16)
    widened = timed.astype(F32)
    scale_inv = lax.rsqrt(jnp.mean(widened * widened, axis=-1, keepdims=True) + 1e-06)
    gained = (widened * gain_ref[...]).astype(BF16)
    tile = (frame_count, slots, channels)
    queries = matmul(gained, wq[...])
    key_rows = matmul(gained, wk[...])
    value_rows = matmul(gained, wv[...])
    queries = (queries * scale_inv).astype(BF16).reshape(tile)
    key_rows = (key_rows * scale_inv).astype(BF16).reshape(tile)
    value_rows = (value_rows * scale_inv).astype(BF16).reshape(tile)
    groups = [slice(g * GROUP, (g + 1) * GROUP) for g in range(slots // GROUP)]
    scores = [
        lax.dot_general(
            queries[:, part].reshape(span, channels),
            key_rows[:, part].reshape(span, channels),
            (((1,), (1,)), ((), ())),
            preferred_element_type=F32,
        )
        for part in groups
    ]
    scores = [score * (1.0 / math.sqrt(channels)) + masked_bias for score in scores]
    peaks = [jnp.max(score, axis=-1, keepdims=True) for score in scores]
    raised = [jnp.exp(score - peak) for score, peak in zip(scores, peaks)]
    totals = [jnp.sum(r, axis=-1, keepdims=True) for r in raised]
    probs = [(r / total).astype(BF16) for r, total in zip(raised, totals)]
    for part, prob in zip(groups, probs):
        mixed = matmul(prob, value_rows[:, part].reshape(span, channels))
        context[:, part] = mixed.astype(BF16).reshape(frame_count, GROUP, channels)
    attended = widened + matmul(context[...].reshape(pixels, channels), wo[...])
    attended = attended.astype(BF16).reshape(tile)

    count = row_count * cols
    for f in range(frame_count):
        gathered = matmul(pick3, attended[f])
        middle = attended[f, 0:taps].astype(F32)
        columns = (gathered[0:taps], middle, gathered[taps : 2 * taps])
        for a in range(3):
            for b in range(3):
                cols3[a, f, :, b * channels : (b + 1) * channels] = columns[b][
                    a * cols : a * cols + count
                ].astype(BF16)
    summed = None
    for a in range(3):
        part = matmul(
            cols3[a].reshape(frame_count * count, 3 * channels),
            w3[a].reshape(3 * channels, channels),
        )
        summed = part if summed is None else summed + part
    out_ref[...] = summed.reshape(frame_count, row_count, cols, channels).astype(BF16)

    for up, down in zip(ups, downs):
        pl.when(row > 0)(up.wait_send)
        pl.when(row < rows_axis - 1)(down.wait_send)
    for exchange in exchanges:
        exchange.wait_send()


def on_device(frames_axis, rows_axis, *args):
    frames_in = args[0]
    norm_gain = args[4]
    local_frames, row_count, width, channels = frames_in.shape
    frame_count = local_frames * frames_axis
    cols = width // frames_axis
    slots = -(-(row_count + 2) * (cols + 2) // GROUP) * GROUP
    args = args[:4] + (norm_gain.reshape(1, channels),) + args[5:]
    any_space = pl.BlockSpec(memory_space=pl.ANY)
    vmem = pl.BlockSpec(memory_space=pltpu.VMEM)
    weight = pltpu.VMEM((3, 3, channels, channels), BF16)
    square = pltpu.VMEM((channels, channels), BF16)
    return pl.pallas_call(
        functools.partial(kernel, frames_axis, rows_axis),
        out_shape=pltpu.VMEM((frame_count, row_count, cols, channels), BF16),
        in_specs=[any_space] * 11,
        out_specs=vmem,
        scratch_shapes=[
            pltpu.VMEM((local_frames, row_count + 2 * HALO, width, channels), BF16),
            pltpu.VMEM((local_frames, row_count + 2 * HALO, width, 3 * channels), BF16),
            pltpu.VMEM((local_frames, row_count + 4, width, 3 * channels), BF16),
            weight,
            weight,
            pltpu.VMEM((3, channels, channels), BF16),
            square,
            square,
            square,
            square,
            weight,
            pltpu.VMEM((local_frames, row_count + 4, width, channels), F32),
            pltpu.VMEM((1, channels), F32),
            pltpu.VMEM((frame_count, frame_count), F32),
            pltpu.VMEM((frames_axis * slots, (row_count + 2) * width), BF16),
            pltpu.VMEM((local_frames, frames_axis, slots, channels), BF16),
            pltpu.VMEM((frame_count + 2, slots, channels), BF16),
            pltpu.VMEM((frame_count, slots, channels), BF16),
            pltpu.VMEM((3, frame_count, row_count * cols, 3 * channels), BF16),
            pltpu.SemaphoreType.DMA((11,)),
            pltpu.SemaphoreType.DMA((local_frames, 2)),
            pltpu.SemaphoreType.DMA((local_frames, 2)),
            pltpu.SemaphoreType.DMA((local_frames, frames_axis)),
            pltpu.SemaphoreType.DMA((local_frames, frames_axis)),
        ],
        compiler_params=pltpu.CompilerParams(
            collective_id=0, has_side_effects=True, vmem_limit_bytes=56 * 1024 * 1024
        ),
    )(*args)


def solution(mesh):
    placed = (P("frame", "row", None, None),) + (P(),) * 10
    return jax.shard_map(
        functools.partial(on_device, mesh.shape["frame"], mesh.shape["row"]),
        mesh=mesh,
        in_specs=placed,
        out_specs=P(None, "row", "frame", None),
        check_vma=False,
    )
```
